256 devices in a mesh: group: 32 (over x, z), members: 8 (over y, core).
Axes of the slice: x: 4, y: 4, z: 8, core: 2. Of those that a mesh axis runs over, the one named last changes fastest.
Arguments:
- out_grad: bfloat16 [32768, 3584], P(('group', 'members')), may hold values from -4 to 4
- hidden_act: bfloat16 [32768, 4, 1024], P(('group', 'members')), may hold values from -0.23925781 to 0.23925781
- gate_weight: bfloat16 [32768, 4], P(('group', 'members')), may hold values from 0.099609375 to 2.5
- routes: int32 [32768, 4], P(('group', 'members')), may hold values from 0 to 127, all different within a row; in each aligned block of 128 rows (0 to 127, 128 to 255, ...) at most 7 rows name the same one
- down_weight: bfloat16 [256, 1024, 1792], P(('group', 'members')), may hold values from -0.1875 to 0.1875
Outputs:
- weight_grad: bfloat16 [256, 1024, 1792], P(('group', 'members'))
- hidden_grad: bfloat16 [32768, 4, 1024], P(('group', 'members'))
- gate_grad: float32 [32768, 4], P(('group', 'members'))
The draws below stay inside these ranges and needn't reach their ends.
Inputs may be any that keep to these rules, and one draw needn't show every extreme that they name: `routes`: each row names 4 different experts. Within the rows of one device no expert is named more than 7 times, and in some device's rows some expert is named exactly 7 times.
All inputs are finite; a program needn't handle non-finite values.
Results may differ from the reference program's by a relative error of at most 0.0085.
Values may be sent and summed in bfloat16 or wider, within the bound.
A program may use at most 128 MiB of HBM per device.

```python
import math
import jax
import jax.numpy as jnp
import numpy as np
from jax import lax

D = 3584
DH = 1792
F = 1024
TOPK = 4
TOK_DEV = 128
EXPERTS = 128
CAP = 7
TOKENS = 32768


def block_levels(own_key, dims, pieces, smallest, top_value):
    factor_of = 1.0
    for position, blocks in pieces:
        steps = jax.random.uniform(jax.random.fold_in(jax.random.fold_in(own_key, 6), position), (blocks,), jnp.float32, smallest / len(pieces), top_value / len(pieces))
        factor_of = factor_of * jnp.repeat(jnp.exp(steps), dims[position] // blocks).reshape((-1,) + (1,) * (len(dims) - 1 - position))
    return factor_of


def assign_block(rng, own, number, rows, count, top, limit, skew):
    sequence = jax.random.permutation(rng, count)
    heavy_load, common = load_shares(count, rows * top, limit, skew, True), load_shares(count, rows * top, limit, skew, False)
    places = jnp.arange(count)

    def named(lengths, turn):
        used = int((lengths > 0).sum())
        fixed = max(1, used // 4)
        moved = fixed + (places - fixed + turn * (used - fixed)) % max(1, count - fixed)
        return jnp.zeros((count,), jnp.int32).at[sequence[jnp.where(places < fixed, places, moved)]].set(jnp.asarray(lengths, jnp.int32))

    lengths = jnp.where(number % 4 == 0, named(heavy_load, number // 4), named(common, number - number // 4 - 1))
    mixed = jax.random.permutation(jax.random.fold_in(own, 3), count)
    donor, taker = mixed[0:count // 2 * 2:2], mixed[1:count // 2 * 2:2]
    slack = jnp.minimum(lengths[donor] - 1, limit - lengths[taker]) // 2
    slack = jnp.where((donor == sequence[0]) | (taker == sequence[0]) | (lengths[taker] == 0), 0, jnp.maximum(slack, 0))
    moved = jax.random.randint(jax.random.fold_in(own, 4), (count // 2,), 0, 1 << 20) % (slack + 1)
    lengths = lengths.at[donor].add(-moved).at[taker].add(moved)
    items = jnp.searchsorted(jnp.cumsum(lengths), jnp.arange(rows * top), side="right").astype(jnp.int32)
    table = items.reshape(top, rows).T
    table = table[jax.random.permutation(jax.random.fold_in(own, 1), rows)]
    turn = jax.random.randint(jax.random.fold_in(own, 2), (rows, 1), 0, top)
    return jnp.take_along_axis(table, (jnp.arange(top)[None, :] + turn) % top, axis=1)


def load_shares(count, total, bound, skew, full):
    loads = [(1 << 20) // math.isqrt(rank ** skew) + 1 for rank in range(1, count + 1)]
    largest = bound if full else min(bound, max(-(-total // count), total * loads[0] // sum(loads)))
    least = 1 if total - largest >= count - 1 else 0
    holding, surplus = [largest] + [least] * (count - 1), total - largest - least * (count - 1)
    while surplus > 0:
        movable = [i for i in range(1, count) if holding[i] < largest] or [i for i in range(1, count) if holding[i] < bound]
        mass, budget = sum([loads[i] for i in movable]), surplus
        for i in movable:
            addition = min(bound - holding[i], max(1, budget * loads[i] // mass), surplus)
            holding[i] = holding[i] + addition
            surplus = surplus - addition
    return np.array(holding)


def centred(key, dims, spread, reach, split=(), held_as=jnp.bfloat16):
    entries = jax.random.normal(key, dims, jnp.float32) * spread
    if len(split) > 0:
        entries = block_levels(key, dims, split, -0.22, 0.18) * entries
    return jnp.clip(entries, min=-reach, max=reach).astype(held_as)


def setup_inputs(seed: int = 0) -> dict:
    key_of = jax.random.split(jax.random.key(seed), 6)
    out_grad = centred(key_of[0], (TOKENS, D), 0.5, 4.0, ((0, 256),))
    hidden_act = centred(key_of[1], (TOKENS, TOPK, F), 0.03, 0.23925781, ((0, 256),))
    gate_weight = jnp.clip(jnp.exp(math.log(2.5) - 3.2227897 * jax.random.uniform(key_of[2], (TOKENS, TOPK), jnp.float32) ** block_levels(key_of[2], (TOKENS, TOPK), ((0, 256),), -0.2, 0.2)), 0.099609375, 2.5).astype(jnp.bfloat16)
    routes_keys = jax.random.split(jax.random.fold_in(key_of[3], 1), TOKENS // TOK_DEV)
    routes_turns = jax.random.permutation(jax.random.fold_in(key_of[3], 3), TOKENS // TOK_DEV)
    routes = jax.vmap(lambda own, number: assign_block(jax.random.fold_in(key_of[3], 2), own, number, TOK_DEV, EXPERTS, TOPK, CAP, 2))(routes_keys, routes_turns).reshape((TOKENS, TOPK))
    down_weight = centred(key_of[4], (2 * EXPERTS, F, DH), F ** -0.5, 0.1875, ((0, 256),))
    return {"out_grad": out_grad, "hidden_act": hidden_act, "gate_weight": gate_weight, "routes": routes, "down_weight": down_weight}


def slot_ranks(blocks):
    onehot = (blocks[..., None] == jnp.arange(EXPERTS, dtype=jnp.int32)).astype(jnp.int32)
    counts = jnp.cumsum(onehot, axis=1)
    return jnp.sum(counts * onehot, axis=-1) - 1


def reference(out_grad, hidden_act, gate_weight, routes, down_weight):
    device_total = TOKENS // TOK_DEV
    slot_total = TOKENS * TOPK
    expert_ids = routes.reshape(slot_total).astype(jnp.int32)
    positions = slot_ranks(expert_ids.reshape(device_total, TOK_DEV * TOPK)).reshape(slot_total)
    device_ids = jnp.arange(slot_total, dtype=jnp.int32) // (TOK_DEV * TOPK)
    sentinel = slot_total
    slot_table = jnp.full((EXPERTS, device_total * CAP), sentinel, jnp.int32)
    slot_table = slot_table.at[expert_ids, device_ids * CAP + positions].set(jnp.arange(slot_total, dtype=jnp.int32))
    grad_padded = jnp.concatenate([out_grad, jnp.zeros((1, D), out_grad.dtype)], axis=0)
    hidden_padded = jnp.concatenate([hidden_act.reshape(slot_total, F), jnp.zeros((1, F), hidden_act.dtype)], axis=0)
    gate_padded = jnp.concatenate([gate_weight.reshape(slot_total), jnp.zeros((1,), gate_weight.dtype)], axis=0)

    def per_expert(totals, expert):
        slot_ids = slot_table[expert]
        token_ids = slot_ids // TOPK
        grad_rows = grad_padded[token_ids]
        hidden_rows = hidden_padded[slot_ids]
        gate_rows = gate_padded[slot_ids].astype(jnp.float32)
        halves = lax.dynamic_slice_in_dim(down_weight, 2 * expert, 2, 0)
        expert_weight = jnp.transpose(halves, (1, 0, 2)).reshape(F, D)
        unscaled = lax.dot_general(grad_rows, expert_weight, (((1,), (1,)), ((), ())), preferred_element_type=jnp.float32)
        rounded = unscaled.astype(jnp.bfloat16)
        hidden_step = (gate_rows[:, None] * rounded.astype(jnp.float32)).astype(jnp.bfloat16)
        gate_step = jnp.sum(rounded.astype(jnp.float32) * hidden_rows.astype(jnp.float32), axis=1)
        scaled = (gate_rows[:, None] * grad_rows.astype(jnp.float32)).astype(jnp.bfloat16)
        weight_step = lax.dot_general(hidden_rows, scaled, (((0,), (0,)), ((), ())), preferred_element_type=jnp.float32).astype(jnp.bfloat16)
        hidden_total = totals[0].at[slot_ids].set(hidden_step)
        gate_total = totals[1].at[slot_ids].set(gate_step)
        return (hidden_total, gate_total), jnp.transpose(weight_step.reshape(F, 2, DH), (1, 0, 2))

    start = (jnp.zeros((slot_total + 1, F), jnp.bfloat16), jnp.zeros((slot_total + 1,), jnp.float32))
    totals, weight_steps = lax.scan(per_expert, start, jnp.arange(EXPERTS, dtype=jnp.int32))
    weight_grad = weight_steps.reshape(2 * EXPERTS, F, DH)
    hidden_grad = totals[0][:slot_total].reshape(TOKENS, TOPK, F)
    gate_grad = totals[1][:slot_total].reshape(TOKENS, TOPK)
    return (weight_grad, hidden_grad, gate_grad)
```

```python
import functools

import jax
import jax.numpy as jnp
from jax import lax
from jax.experimental import pallas as pl
from jax.experimental.pallas import tpu as pltpu
from jax.sharding import PartitionSpec as P

MESH = pl.DeviceIdType.MESH
NX = 4
PAD = 8
BLK = 2 * PAD


class Place:
    def __init__(self, groups, members):
        self.nx = NX
        self.nz = groups // NX
        self.ny = members // 2
        self.plane = self.nx * self.ny
        g = lax.axis_index("group")
        m = lax.axis_index("members")
        self.x = g // self.nz
        self.z = lax.rem(g, self.nz)
        self.y = m // 2
        self.c = lax.rem(m, 2)
        self.a = self.x * self.ny + self.y

    def dev(self, x, z, y, c):
        return (x * self.nz + z, y * 2 + c)

    def sibling(self):
        return self.dev(self.x, self.z, self.y, 1 - self.c)

    def along_z(self, step):
        z = lax.rem(self.z + step + self.nz, self.nz)
        return z, self.dev(self.x, z, self.y, self.c)

    def in_plane(self, i):
        x = lax.rem(self.x + i // self.ny, self.nx)
        y = lax.rem(self.y + lax.rem(i, self.ny), self.ny)
        return x * self.ny + y, self.dev(x, self.z, y, self.c)

    def greet(self):
        barrier = pltpu.get_barrier_semaphore()
        pl.semaphore_signal(barrier, inc=1, device_id=self.sibling(), device_id_type=MESH)

        @pl.loop(1, self.nz)
        def _(j):
            pl.semaphore_signal(
                barrier, inc=1, device_id=self.along_z(j)[1], device_id_type=MESH
            )

        @pl.loop(1, self.plane)
        def _(i):
            pl.semaphore_signal(
                barrier, inc=1, device_id=self.in_plane(i)[1], device_id_type=MESH
            )

        pl.semaphore_wait(barrier, self.nz + self.plane - 1)


def remote(src, dst, ssem, rsem, device):
    return pltpu.make_async_remote_copy(
        src_ref=src, dst_ref=dst, send_sem=ssem, recv_sem=rsem, device_id=device, device_id_type=MESH
    )


def route_hits(ids, rows):
    parts = []
    for core in range(2):
        for k in range(ids.shape[1] // 2):
            hit = rows == ids[core, k : k + 1, :]
            parts.append(jnp.where(hit, 1.0, 0.0).astype(jnp.bfloat16))
    return jnp.concatenate(parts, axis=1)


def token_hits(ids, rows):
    parts = []
    for core in range(2):
        hit = rows == ids[core, 0:1, :]
        for k in range(1, ids.shape[1] // 2):
            hit = hit | (rows == ids[core, k : k + 1, :])
        parts.append(jnp.where(hit, 1.0, 0.0).astype(jnp.bfloat16))
    return jnp.concatenate(parts, axis=1)


def dispatch_kernel(
    groups, members,
    og, hs, sid,
    rb, hf, ids_out,
    gat, ids, sb, h0, hsend, hmid,
    x_s, x_r, x_l, ag_s, ag_r, agm_s, agm_r,
    p_s, p_r, p_l, hp_s, hp_r, hp_l, hz_s, hz_r, hz_l, hx_s, hx_r, out_l,
):
    me = Place(groups, members)
    nz, plane = me.nz, me.plane
    half_d = gat.shape[2]
    half_f = h0.shape[1]
    tok = og.shape[0]
    n_routes = hs.shape[0]
    z, c, a = me.z, me.c, me.a
    steps = nz // 2
    chunk = plane * BLK

    me.greet()

    def cols(n, which):
        return pl.ds(pl.multiple_of(which * n, n), n)

    own = [
        (og.at[:, cols(half_d, c)], gat.at[z, pl.ds(pl.multiple_of(c * tok, tok), tok)]),
        (hs.at[:, cols(half_f, c)], h0.at[pl.ds(pl.multiple_of(c * n_routes, n_routes), n_routes)]),
        (sid, ids.at[z, c]),
    ]
    away = [
        og.at[:, cols(half_d, 1 - c)],
        hs.at[:, cols(half_f, 1 - c)],
        sid,
    ]
    give = [
        remote(src, dst, x_s.at[i], x_r.at[i], me.sibling())
        for i, (src, (_, dst)) in enumerate(zip(away, own))
    ]
    keep = [pltpu.make_async_copy(src, dst, x_l.at[i]) for i, (src, dst) in enumerate(own)]
    for op in give:
        op.start()
    for op in keep:
        op.start()
    for op in keep:
        op.wait()
    for op in give:
        op.wait_recv()

    def ring(way, step, half):
        block = lax.rem(z - step + nz, nz) if way == 0 else lax.rem(z + step, nz)
        _, target = me.along_z(1 if way == 0 else -1)
        rows = gat.at[block, half * tok : (half + 1) * tok]
        table = ids.at[block, half]
        return (
            remote(rows, rows, ag_s.at[way, step, half], ag_r.at[way, step, half], target),
            remote(table, table, agm_s.at[way, step, half], agm_r.at[way, step, half], target),
        )

    def ring_start(way, step, half):
        for op in ring(way, step, half):
            op.start()

    def ring_arrive(way, step, half):
        for op in ring(way, step, half):
            op.wait_recv()

    for half in range(2):
        ring_start(0, 0, half)
        ring_start(1, 0, half)

    def spread(block):
        rows = lax.broadcasted_iota(jnp.int32, (chunk, 1), 0) + z * chunk
        hits = token_hits(ids[block], rows)
        width = half_d // 7 if half_d % (7 * 128) == 0 else half_d
        for t in range(half_d // width):
            picked = jnp.dot(
                hits, gat[block, :, t * width : (t + 1) * width], preferred_element_type=jnp.float32
            )
            sb[block, :, :, t * width : (t + 1) * width] = picked.astype(jnp.bfloat16).reshape(
                plane, BLK, width
            )

        @pl.loop(1, plane)
        def _(i):
            q, target = me.in_plane(i)
            remote(sb.at[block, q], rb.at[block, a], p_s.at[block], p_r.at[block], target).start()

        pltpu.make_async_copy(sb.at[block, a], rb.at[block, a], p_l.at[block]).start()

    def spread_hidden():
        per_x = me.ny * nz * BLK

        @pl.loop(0, me.nx)
        def _(dx):
            row = lax.broadcasted_iota(jnp.int32, (per_x, 1), 0)
            xq = lax.rem(me.x + dx, me.nx)
            slot = lax.rem(row, BLK)
            zq = lax.rem(row // BLK, nz)
            yq = row // (BLK * nz)
            rows = zq * chunk + (xq * me.ny + yq) * BLK + slot
            hits = route_hits(ids[z], rows)
            picked = jnp.dot(hits, h0[...], preferred_element_type=jnp.float32)
            hsend[pl.ds(xq * me.ny, me.ny)] = picked.astype(jnp.bfloat16).reshape(
                me.ny, nz, BLK, half_f
            )

        @pl.loop(1, plane)
        def _(i):
            q, target = me.in_plane(i)
            remote(hsend.at[q], hmid.at[a], hp_s.at[0], hp_r.at[0], target).start()

        pltpu.make_async_copy(hsend.at[a], hmid.at[a], hp_l.at[0]).start()

    def hidden_arrive():
        pltpu.make_async_copy(
            hmid.at[pl.ds(0, plane - 1)], hmid.at[pl.ds(0, plane - 1)], hp_r.at[0]
        ).wait()
        pltpu.make_async_copy(hsend.at[a], hmid.at[a], hp_l.at[0]).wait()

    def hidden_hop(j):
        to, target = me.along_z(j)
        return remote(hmid.at[:, to], hf.at[c, z], hz_s.at[j], hz_r.at[j], target)

    def hidden_share(j):
        frm = lax.rem(z - j + nz, nz)
        return remote(hf.at[c, frm], hf.at[c, frm], hx_s.at[j], hx_r.at[j], me.sibling())

    spread(z)
    spread_hidden()

    @pl.loop(1, nz)
    def _(o):
        step = (o - 1) // 2
        up = lax.rem(o, 2) == 1
        last = o == nz - 1

        @pl.when(last)
        def _():
            ring_arrive(0, steps - 1, 0)
            ring_arrive(1, steps - 1, 1)

        @pl.when(jnp.logical_and(up, jnp.logical_not(last)))
        def _():
            ring_arrive(0, step, 0)
            ring_arrive(0, step, 1)
            ring_start(0, step + 1, 0)

            @pl.when(step + 1 < steps - 1)
            def _():
                ring_start(0, step + 1, 1)

        @pl.when(jnp.logical_not(up))
        def _():
            ring_arrive(1, step, 0)
            ring_arrive(1, step, 1)
            ring_start(1, step + 1, 1)

            @pl.when(step + 1 < steps - 1)
            def _():
                ring_start(1, step + 1, 0)

        block = jnp.where(up, lax.rem(z - 1 - step + nz, nz), lax.rem(z + 1 + step, nz))
        spread(block)

        @pl.when(o == nz - 2)
        def _():
            hidden_arrive()
            pltpu.make_async_copy(hmid.at[:, z], hf.at[c, z], hz_l.at[0]).start()

            @pl.loop(1, nz)
            def _(j):
                hidden_hop(j).start()

    pltpu.make_async_copy(hmid.at[:, z], hf.at[c, z], hz_l.at[0]).wait()
    hidden_share(0).start()

    @pl.loop(1, nz)
    def _(j):
        hidden_hop(j).wait_recv()
        hidden_share(j).start()

    table = pltpu.make_async_copy(ids.at[z], ids_out, out_l.at[0])
    table.start()
    table.wait()

    @pl.loop(0, nz)
    def _(block):
        pltpu.make_async_copy(
            rb.at[block, pl.ds(0, plane - 1)], rb.at[block, pl.ds(0, plane - 1)], p_r.at[block]
        ).wait()
        pltpu.make_async_copy(
            sb.at[block, pl.ds(0, plane - 1)], sb.at[block, pl.ds(0, plane - 1)], p_s.at[block]
        ).wait()
        pltpu.make_async_copy(sb.at[block, a], rb.at[block, a], p_l.at[block]).wait()
        hidden_share(block).wait()

    @pl.loop(1, nz)
    def _(j):
        hidden_hop(j).wait_send()

    pltpu.make_async_copy(
        hsend.at[pl.ds(0, plane - 1)], hsend.at[pl.ds(0, plane - 1)], hp_s.at[0]
    ).wait()
    for op in give:
        op.wait_send()
    for step in range(steps):
        for way in range(2):
            for half in range(2):
                if step < steps - 1 or way == half:
                    for op in ring(way, step, half):
                        op.wait_send()


def return_kernel(
    groups, members,
    part, ids_in,
    out,
    own, got, ret, rmid, rr, acc, both, ids,
    o_l, e_s, e_r, p_s, p_r, p_l, z_s, z_r, z_l, u_s, u_r, u_l, i_l,
):
    me = Place(groups, members)
    nz, plane = me.nz, me.plane
    z, c, a = me.z, me.c, me.a
    half_f = own.shape[3]
    chunk = plane * BLK
    n_routes = both.shape[1]

    me.greet()
    table = pltpu.make_async_copy(ids_in, ids, i_l.at[0])
    table.start()

    def cols(which):
        return pl.ds(pl.multiple_of(which * half_f, half_f), half_f)

    def order(o):
        return lax.rem(z + nz // 2 + o, nz)

    def mine(o):
        b = order(o)
        return pltpu.make_async_copy(part.at[b, :, :, cols(c)], own.at[b], o_l.at[b])

    def other(o):
        b = order(o)
        return remote(part.at[b, :, :, cols(1 - c)], got.at[b], e_s.at[b], e_r.at[b], me.sibling())

    @pl.loop(0, nz)
    def _(o):
        mine(o).start()
        other(o).start()

    table.wait()

    def hop(b):
        return remote(rmid.at[b], rr.at[z], z_s.at[b], z_r.at[z], me.dev(me.x, b, me.y, c))

    @pl.loop(0, nz)
    def _(o):
        b = order(o)
        mine(o).wait()
        other(o).wait_recv()
        ret[b] = (own[b] + got[b]).astype(jnp.bfloat16)

        @pl.loop(1, plane)
        def _(i):
            q, target = me.in_plane(i)
            remote(ret.at[b, q], rmid.at[b, a], p_s.at[b], p_r.at[b], target).start()

        pltpu.make_async_copy(ret.at[b, a], rmid.at[b, a], p_l.at[b]).start()

    @pl.loop(0, nz)
    def _(o):
        b = order(o)
        pltpu.make_async_copy(
            rmid.at[b, pl.ds(0, plane - 1)], rmid.at[b, pl.ds(0, plane - 1)], p_r.at[b]
        ).wait()
        pltpu.make_async_copy(ret.at[b, a], rmid.at[b, a], p_l.at[b]).wait()

        @pl.when(b != z)
        def _():
            hop(b).start()

        @pl.when(b == z)
        def _():
            pltpu.make_async_copy(rmid.at[b], rr.at[z], z_l.at[0]).start()

    acc[...] = jnp.zeros_like(acc)

    def take(b):
        rows = lax.broadcasted_iota(jnp.int32, (chunk, 1), 0) + b * chunk
        hits = route_hits(ids[...], rows)
        acc[...] += lax.dot_general(
            hits,
            rr[b].reshape(chunk, half_f),
            (((0,), (0,)), ((), ())),
            preferred_element_type=jnp.float32,
        )

    pltpu.make_async_copy(rmid.at[z], rr.at[z], z_l.at[0]).wait()
    take(z)

    @pl.loop(1, nz)
    def _(j):
        b = lax.rem(z + j, nz)
        pltpu.make_async_copy(rr.at[b], rr.at[b], z_r.at[b]).wait()
        take(b)

    both[...] = acc[...].astype(jnp.bfloat16).reshape(both.shape)
    give = remote(both.at[1 - c], out.at[c], u_s.at[0], u_r.at[0], me.sibling())
    keep = pltpu.make_async_copy(both.at[c], out.at[c], u_l.at[0])
    give.start()
    keep.start()
    keep.wait()
    give.wait()

    @pl.loop(0, nz)
    def _(b):
        other(b).wait_send()
        pltpu.make_async_copy(
            ret.at[b, pl.ds(0, plane - 1)], ret.at[b, pl.ds(0, plane - 1)], p_s.at[b]
        ).wait()

        @pl.when(b != z)
        def _():
            hop(b).wait_send()


def dispatch(groups, members, og, hs, sid):
    nz, ny = groups // NX, members // 2
    plane = NX * ny
    tok, d = og.shape
    n_routes, f = hs.shape
    dma = pltpu.SemaphoreType.DMA
    any_ = pl.BlockSpec(memory_space=pl.ANY)
    bf = jnp.bfloat16
    steps = nz // 2
    return pl.pallas_call(
        functools.partial(dispatch_kernel, groups, members),
        name="dispatch",
        out_shape=(
            jax.ShapeDtypeStruct((nz, plane, BLK, d // 2), bf),
            jax.ShapeDtypeStruct((2, nz, plane, BLK, f // 2), bf),
            jax.ShapeDtypeStruct((2,) + sid.shape, jnp.int32),
        ),
        in_specs=[any_] * 3,
        out_specs=(any_,) * 3,
        scratch_shapes=[
            pltpu.VMEM((nz, 2 * tok, d // 2), bf),
            pltpu.VMEM((nz, 2) + sid.shape, jnp.int32),
            pltpu.VMEM((nz, plane, BLK, d // 2), bf),
            pltpu.VMEM((2 * n_routes, f // 2), bf),
            pltpu.VMEM((plane, nz, BLK, f // 2), bf),
            pltpu.VMEM((plane, nz, BLK, f // 2), bf),
            dma((3,)), dma((3,)), dma((3,)),
            dma((2, steps, 2)), dma((2, steps, 2)), dma((2, steps, 2)), dma((2, steps, 2)),
            dma((nz,)), dma((nz,)), dma((nz,)),
            dma((1,)), dma((1,)), dma((1,)),
            dma((nz,)), dma((nz,)), dma((1,)),
            dma((nz,)), dma((nz,)), dma((1,)),
        ],
        compiler_params=pltpu.CompilerParams(
            collective_id=0, has_side_effects=True, vmem_limit_bytes=60 << 20
        ),
    )(og, hs, sid)


def give_back(groups, members, part, ids):
    nz, ny = groups // NX, members // 2
    plane = NX * ny
    half_f = part.shape[3] // 2
    tok = ids.shape[2]
    n_routes = tok * (ids.shape[1] // 2)
    dma = pltpu.SemaphoreType.DMA
    any_ = pl.BlockSpec(memory_space=pl.ANY)
    bf = jnp.bfloat16
    return pl.pallas_call(
        functools.partial(return_kernel, groups, members),
        name="give_back",
        out_shape=jax.ShapeDtypeStruct((2, n_routes, half_f), bf),
        in_specs=[any_] * 2,
        out_specs=any_,
        scratch_shapes=[
            pltpu.VMEM((nz, plane, BLK, half_f), jnp.float32),
            pltpu.VMEM((nz, plane, BLK, half_f), jnp.float32),
            pltpu.VMEM((nz, plane, BLK, half_f), bf),
            pltpu.VMEM((nz, plane, BLK, half_f), bf),
            pltpu.VMEM((nz, plane, BLK, half_f), bf),
            pltpu.VMEM((2 * n_routes, half_f), jnp.float32),
            pltpu.VMEM((2, n_routes, half_f), bf),
            pltpu.VMEM(ids.shape, jnp.int32),
            dma((nz,)), dma((nz,)), dma((nz,)),
            dma((nz,)), dma((nz,)), dma((nz,)),
            dma((nz,)), dma((nz,)), dma((1,)),
            dma((1,)), dma((1,)), dma((1,)), dma((1,)),
        ],
        compiler_params=pltpu.CompilerParams(
            collective_id=1, has_side_effects=True, vmem_limit_bytes=60 << 20
        ),
    )(part, ids)


def local(out_grad, hidden_act, gate_weight, routes, down_weight):
    groups = lax.axis_size("group")
    members = lax.axis_size("members")
    nz, ny = groups // NX, members // 2
    plane = NX * ny
    tok, d = out_grad.shape
    top, f = hidden_act.shape[1:]
    rows = nz * plane * BLK
    core = lax.rem(lax.axis_index("members"), 2)

    expert = routes.T.reshape(-1)
    earlier = jnp.arange(top * tok)[None, :] < jnp.arange(top * tok)[:, None]
    same = expert[None, :] == expert[:, None]
    rank = jnp.sum((same & earlier).astype(jnp.int32), axis=1)
    ex, ez, ey = expert // (nz * ny), (expert // ny) % nz, expert % ny
    slot = (ez * plane + ex * ny + ey) * BLK + core * PAD + rank
    sid = jnp.concatenate([slot.reshape(top, tok), jnp.full((top, tok), -1, jnp.int32)], axis=0)

    gate = gate_weight.astype(jnp.float32)
    hs = (gate[:, :, None] * hidden_act.astype(jnp.float32)).astype(jnp.bfloat16)
    hs = jnp.transpose(hs, (1, 0, 2)).reshape(top * tok, f)

    rb, hf, ids = dispatch(groups, members, out_grad, hs, sid)
    grad_in = rb.reshape(rows, d // 2)
    part = lax.dot_general(
        grad_in, down_weight[0], (((1,), (1,)), ((), ())), preferred_element_type=jnp.float32
    )
    back = give_back(groups, members, part.reshape(nz, plane, BLK, f), ids)
    weight_grad = lax.dot_general(
        hf.reshape(2, rows, f // 2), grad_in, (((1,), (0,)), ((), ())),
        preferred_element_type=jnp.float32,
    ).astype(jnp.bfloat16).reshape(1, f, d // 2)

    unscaled = jnp.transpose(back.reshape(2, top, tok, f // 2), (2, 1, 0, 3)).reshape(tok, top, f)
    wide = unscaled.astype(jnp.float32)
    hidden_grad = (gate[:, :, None] * wide).astype(jnp.bfloat16)
    gate_grad = jnp.sum(wide * hidden_act.astype(jnp.float32), axis=2)
    return weight_grad, hidden_grad, gate_grad


def solution(mesh):
    both = ("group", "members")
    return jax.shard_map(
        local,
        mesh=mesh,
        in_specs=(P(both, None), P(both, None, None), P(both, None), P(both, None), P(both, None, None)),
        out_specs=(P(both, None, None), P(both, None, None), P(both, None)),
        check_vma=False,
    )
```

```python
import functools

import jax
import jax.numpy as jnp
from jax import lax
from jax.experimental import pallas as pl
from jax.experimental.pallas import tpu as pltpu
from jax.sharding import PartitionSpec as P

MESH = pl.DeviceIdType.MESH
NX = 4
PAD = 8
BLK = 2 * PAD


class Place:
    def __init__(self, groups, members):
        self.nx = NX
        self.nz = groups // NX
        self.ny = members // 2
        self.plane = self.nx * self.ny
        g = lax.axis_index("group")
        m = lax.axis_index("members")
        self.x = g // self.nz
        self.z = lax.rem(g, self.nz)
        self.y = m // 2
        self.c = lax.rem(m, 2)
        self.a = self.x * self.ny + self.y

    def dev(self, x, z, y, c):
        return (x * self.nz + z, y * 2 + c)

    def sibling(self):
        return self.dev(self.x, self.z, self.y, 1 - self.c)

    def along_z(self, step):
        z = lax.rem(self.z + step + self.nz, self.nz)
        return z, self.dev(self.x, z, self.y, self.c)

    def in_plane(self, i):
        x = lax.rem(self.x + i // self.ny, self.nx)
        y = lax.rem(self.y + lax.rem(i, self.ny), self.ny)
        return x * self.ny + y, self.dev(x, self.z, y, self.c)

    def greet(self):
        barrier = pltpu.get_barrier_semaphore()
        pl.semaphore_signal(barrier, inc=1, device_id=self.sibling(), device_id_type=MESH)

        @pl.loop(1, self.nz)
        def _(j):
            pl.semaphore_signal(
                barrier, inc=1, device_id=self.along_z(j)[1], device_id_type=MESH
            )

        @pl.loop(1, self.plane)
        def _(i):
            pl.semaphore_signal(
                barrier, inc=1, device_id=self.in_plane(i)[1], device_id_type=MESH
            )

        pl.semaphore_wait(barrier, self.nz + self.plane - 1)


def remote(src, dst, ssem, rsem, device):
    return pltpu.make_async_remote_copy(
        src_ref=src, dst_ref=dst, send_sem=ssem, recv_sem=rsem, device_id=device, device_id_type=MESH
    )


def route_hits(ids, rows):
    parts = []
    for core in range(2):
        for k in range(ids.shape[1] // 2):
            hit = rows == ids[core, k : k + 1, :]
            parts.append(jnp.where(hit, 1.0, 0.0).astype(jnp.bfloat16))
    return jnp.concatenate(parts, axis=1)


def token_hits(ids, rows):
    parts = []
    for core in range(2):
        hit = rows == ids[core, 0:1, :]
        for k in range(1, ids.shape[1] // 2):
            hit = hit | (rows == ids[core, k : k + 1, :])
        parts.append(jnp.where(hit, 1.0, 0.0).astype(jnp.bfloat16))
    return jnp.concatenate(parts, axis=1)


def kernel(
    groups, members,
    og, hs, sid, w_in,
    wg, out,
    gat, ids, sb, rb, w, h0, hsend, hmid, hf, lt, part, got, ret, rmid, rr, acc, both,
    x_s, x_r, x_l, ag_s, ag_r, agm_s, agm_r,
    p_s, p_r, p_l, hp_s, hp_r, hp_l, hz_s, hz_r, hz_l, hx_s, hx_r,
    e_s, e_r, r_s, r_r, r_l, z_s, z_r, z_l, u_s, u_r, u_l, w_l, wg_l,
):
    me = Place(groups, members)
    nz, plane = me.nz, me.plane
    half_d = gat.shape[2]
    half_f = h0.shape[1]
    tok = og.shape[0]
    n_routes = hs.shape[0]
    z, c, a = me.z, me.c, me.a
    steps = nz // 2
    chunk = plane * BLK
    f32, bf = jnp.float32, jnp.bfloat16
    w_tiles, w_rows = w.shape[0], w.shape[1]

    me.greet()

    def cols(n, which):
        return pl.ds(pl.multiple_of(which * n, n), n)

    def block_of(o):
        down = lax.rem(o, 2) == 0
        step = lax.div(o + 1, 2)
        return lax.rem(jnp.where(down, z + step, z - step + nz), nz)

    own = [
        (og.at[:, cols(half_d, c)], gat.at[z, pl.ds(pl.multiple_of(c * tok, tok), tok)]),
        (sid, ids.at[z, c]),
        (hs.at[:, cols(half_f, c)], h0.at[pl.ds(pl.multiple_of(c * n_routes, n_routes), n_routes)]),
    ]
    away = [og.at[:, cols(half_d, 1 - c)], sid, hs.at[:, cols(half_f, 1 - c)]]
    give = [
        remote(src, dst, x_s.at[i], x_r.at[i], me.sibling())
        for i, (src, (_, dst)) in enumerate(zip(away, own))
    ]
    keep = [pltpu.make_async_copy(src, dst, x_l.at[i]) for i, (src, dst) in enumerate(own)]
    for op in give:
        op.start()
    for op in keep:
        op.start()
    weights = pltpu.make_async_copy(w_in, w, w_l.at[0])
    weights.start()

    def ring(way, step, half):
        block = lax.rem(z - step + nz, nz) if way == 0 else lax.rem(z + step, nz)
        _, target = me.along_z(1 if way == 0 else -1)
        rows = gat.at[block, pl.ds(pl.multiple_of(half * tok, tok), tok)]
        table = ids.at[block, half]
        return (
            remote(rows, rows, ag_s.at[way, step, half], ag_r.at[way, step, half], target),
            remote(table, table, agm_s.at[way, step, half], agm_r.at[way, step, half], target),
        )

    def ring_start(way, step, half):
        for op in ring(way, step, half):
            op.start()

    def ring_arrive(way, step, half):
        for op in ring(way, step, half):
            op.wait_recv()

    keep[0].wait()
    keep[1].wait()
    ring_start(0, 0, c)
    ring_start(1, 0, c)
    give[0].wait_recv()
    give[1].wait_recv()
    ring_start(0, 0, 1 - c)
    ring_start(1, 0, 1 - c)

    def spread(block):
        rows = lax.broadcasted_iota(jnp.int32, (chunk, 1), 0) + z * chunk
        hits = token_hits(ids[block], rows)
        width = half_d // 7 if half_d % (7 * 128) == 0 else half_d
        for t in range(half_d // width):
            picked = jnp.dot(
                hits, gat[block, :, t * width : (t + 1) * width], preferred_element_type=f32
            )
            sb[block, :, :, t * width : (t + 1) * width] = picked.astype(bf).reshape(
                plane, BLK, width
            )

        @pl.loop(1, plane)
        def _(i):
            q, target = me.in_plane(i)
            remote(sb.at[block, q], rb.at[block, a], p_s.at[block], p_r.at[block], target).start()

        pltpu.make_async_copy(sb.at[block, a], rb.at[block, a], p_l.at[block]).start()

    def spread_hidden():
        per_x = me.ny * nz * BLK

        @pl.loop(0, me.nx)
        def _(dx):
            row = lax.broadcasted_iota(jnp.int32, (per_x, 1), 0)
            xq = lax.rem(me.x + dx, me.nx)
            slot = lax.rem(row, BLK)
            zq = lax.rem(row // BLK, nz)
            yq = row // (BLK * nz)
            rows = zq * chunk + (xq * me.ny + yq) * BLK + slot
            hits = route_hits(ids[z], rows)
            picked = jnp.dot(hits, h0[...], preferred_element_type=f32)
            hsend[pl.ds(xq * me.ny, me.ny)] = picked.astype(bf).reshape(me.ny, nz, BLK, half_f)

        @pl.loop(1, plane)
        def _(i):
            q, target = me.in_plane(i)
            remote(hsend.at[q], hmid.at[a], hp_s.at[0], hp_r.at[0], target).start()

        pltpu.make_async_copy(hsend.at[a], hmid.at[a], hp_l.at[0]).start()

    def hidden_arrive():
        pltpu.make_async_copy(
            hmid.at[pl.ds(0, plane - 1)], hmid.at[pl.ds(0, plane - 1)], hp_r.at[0]
        ).wait()
        pltpu.make_async_copy(hsend.at[a], hmid.at[a], hp_l.at[0]).wait()

    def hidden_hop(j):
        to, target = me.along_z(j)
        return remote(hmid.at[:, to], hf.at[c, z], hz_s.at[j], hz_r.at[j], target)

    def hidden_share(j):
        frm = lax.rem(z - j + nz, nz)
        return remote(hf.at[c, frm], hf.at[c, frm], hx_s.at[j], hx_r.at[j], me.sibling())

    def swap(b):
        return remote(
            part.at[b, 1 - c], got.at[b], e_s.at[b], e_r.at[b], me.sibling()
        )

    def multiply(o):
        b = block_of(o)
        pltpu.make_async_copy(
            rb.at[b, pl.ds(0, plane - 1)], rb.at[b, pl.ds(0, plane - 1)], p_r.at[b]
        ).wait()
        pltpu.make_async_copy(sb.at[b, a], rb.at[b, a], p_l.at[b]).wait()
        for t in range(w_tiles):
            at = t * w_rows
            part[b, at // half_f, :, at % half_f : at % half_f + w_rows] = lax.dot_general(
                rb[b].reshape(chunk, half_d),
                w[t],
                (((1,), (1,)), ((), ())),
                preferred_element_type=f32,
            )
        swap(b).start()

    def combine(o):
        b = block_of(o)
        swap(b).wait_recv()
        ret[b] = (part[b, c] + got[b]).astype(bf).reshape(plane, BLK, half_f)

        @pl.loop(1, plane)
        def _(i):
            q, target = me.in_plane(i)
            remote(ret.at[b, q], rmid.at[b, a], r_s.at[b], r_r.at[b], target).start()

        pltpu.make_async_copy(ret.at[b, a], rmid.at[b, a], r_l.at[b]).start()

    def hop(b):
        return remote(rmid.at[b], rr.at[z], z_s.at[b], z_r.at[z], me.dev(me.x, b, me.y, c))

    def pass_on(o):
        b = block_of(o)
        pltpu.make_async_copy(
            rmid.at[b, pl.ds(0, plane - 1)], rmid.at[b, pl.ds(0, plane - 1)], r_r.at[b]
        ).wait()
        pltpu.make_async_copy(ret.at[b, a], rmid.at[b, a], r_l.at[b]).wait()

        @pl.when(b != z)
        def _():
            hop(b).start()

        @pl.when(b == z)
        def _():
            pltpu.make_async_copy(rmid.at[b], rr.at[z], z_l.at[0]).start()

    spread(z)
    keep[2].wait()
    give[2].wait_recv()
    spread_hidden()
    weights.wait()

    @pl.loop(0, 2 * (steps - 1))
    def _(n):
        step = n // 2
        half = lax.rem(n, 2)
        lo = jnp.maximum(2 * step - 3, 0)
        hi = jnp.maximum(2 * step - 1, 0)
        ring_arrive(0, step, half)

        @pl.when(jnp.logical_or(step + 1 < steps - 1, half == 0))
        def _():
            ring_start(0, step + 1, half)

        ring_arrive(1, step, half)

        @pl.when(jnp.logical_or(step + 1 < steps - 1, half == 1))
        def _():
            ring_start(1, step + 1, half)

        @pl.when(half == 1)
        def _():
            @pl.loop(2 * step + 1, 2 * step + 3)
            def _(o):
                spread(block_of(o))

            @pl.loop(lo, hi)
            def _(o):
                combine(o)

        @pl.when(half == 0)
        def _():
            @pl.loop(lo, hi)
            def _(o):
                multiply(o)

    hidden_arrive()
    pltpu.make_async_copy(hmid.at[:, z], hf.at[c, z], hz_l.at[0]).start()

    @pl.loop(1, nz)
    def _(j):
        hidden_hop(j).start()

    ring_arrive(0, steps - 1, 0)
    ring_arrive(1, steps - 1, 1)
    spread(block_of(nz - 1))
    first = max(2 * steps - 5, 0)

    @pl.loop(first, nz + 3)
    def _(i):
        @pl.when(i < nz)
        def _():
            multiply(i)

        @pl.when(jnp.logical_and(i > first, i < nz + 1))
        def _():
            combine(i - 1)

        @pl.when(i >= 3)
        def _():
            pass_on(i - 3)

    pltpu.make_async_copy(hmid.at[:, z], hf.at[c, z], hz_l.at[0]).wait()
    hidden_share(0).start()

    @pl.loop(1, nz)
    def _(j):
        hidden_hop(j).wait_recv()
        hidden_share(j).start()

    for step in range(steps):
        for way in range(2):
            for half in range(2):
                if step < steps - 1 or way == half:
                    for op in ring(way, step, half):
                        op.wait_send()

    @pl.loop(0, nz)
    def _(j):
        hidden_share(j).wait()

    f_rows = lt.shape[0]
    per_half = half_f // f_rows
    d_cols = 256

    @pl.loop(0, 2 * per_half)
    def _(i):
        h = i // per_half
        at = pl.multiple_of(lax.rem(i, per_half) * f_rows, f_rows)
        lt[...] = jnp.transpose(hf[h, :, :, :, pl.ds(at, f_rows)].reshape(nz * chunk, f_rows))

        @pl.loop(0, half_d // d_cols)
        def _(t):
            span = pl.ds(pl.multiple_of(t * d_cols, d_cols), d_cols)
            tile = jnp.dot(
                lt[...], rb[:, :, :, span].reshape(nz * chunk, d_cols), preferred_element_type=f32
            )
            gat[i, pl.ds(0, f_rows), span] = tile.astype(bf)

        pltpu.make_async_copy(
            gat.at[i, pl.ds(0, f_rows)], wg.at[pl.ds(i * f_rows, f_rows)], wg_l.at[i]
        ).start()

    acc[...] = jnp.zeros_like(acc)
    pltpu.make_async_copy(rmid.at[z], rr.at[z], z_l.at[0]).wait()

    @pl.loop(0, nz)
    def _(o):
        b = block_of(o)

        @pl.when(o > 0)
        def _():
            pltpu.make_async_copy(rr.at[b], rr.at[b], z_r.at[b]).wait()

        rows = lax.broadcasted_iota(jnp.int32, (chunk, 1), 0) + b * chunk
        hits = route_hits(ids[z], rows)
        acc[...] += lax.dot_general(
            hits,
            rr[b].reshape(chunk, half_f),
            (((0,), (0,)), ((), ())),
            preferred_element_type=f32,
        )

    both[...] = acc[...].astype(bf).reshape(both.shape)
    last = remote(both.at[1 - c], out.at[c], u_s.at[0], u_r.at[0], me.sibling())
    mine = pltpu.make_async_copy(both.at[c], out.at[c], u_l.at[0])
    last.start()
    mine.start()

    @pl.loop(0, nz)
    def _(b):
        for buf, sem in ((sb, p_s), (ret, r_s)):
            pltpu.make_async_copy(
                buf.at[b, pl.ds(0, plane - 1)], buf.at[b, pl.ds(0, plane - 1)], sem.at[b]
            ).wait()
        swap(b).wait_send()

        @pl.when(b != z)
        def _():
            hop(b).wait_send()

    @pl.loop(1, nz)
    def _(j):
        hidden_hop(j).wait_send()

    pltpu.make_async_copy(
        hsend.at[pl.ds(0, plane - 1)], hsend.at[pl.ds(0, plane - 1)], hp_s.at[0]
    ).wait()
    for op in give:
        op.wait_send()

    @pl.loop(0, 2 * per_half)
    def _(i):
        pltpu.make_async_copy(
            gat.at[i, pl.ds(0, f_rows)], wg.at[pl.ds(i * f_rows, f_rows)], wg_l.at[i]
        ).wait()

    mine.wait()
    last.wait()


def exchange(groups, members, og, hs, sid, weight):
    nz, ny = groups // NX, members // 2
    plane = NX * ny
    tok, d = og.shape
    n_routes, f = hs.shape
    half_d, half_f = d // 2, f // 2
    chunk = plane * BLK
    dma = pltpu.SemaphoreType.DMA
    any_ = pl.BlockSpec(memory_space=pl.ANY)
    bf, f32 = jnp.bfloat16, jnp.float32
    steps = nz // 2
    w_rows = min(256, half_f)
    f_rows = min(256, half_f)
    vm = pltpu.VMEM
    return pl.pallas_call(
        functools.partial(kernel, groups, members),
        name="exchange",
        out_shape=(
            jax.ShapeDtypeStruct((f, half_d), bf),
            jax.ShapeDtypeStruct((2, n_routes, half_f), bf),
        ),
        in_specs=[any_] * 4,
        out_specs=(any_,) * 2,
        scratch_shapes=[
            vm((nz, 2 * tok, half_d), bf),
            vm((nz, 2) + sid.shape, jnp.int32),
            vm((nz, plane, BLK, half_d), bf),
            vm((nz, plane, BLK, half_d), bf),
            vm((f // w_rows, w_rows, half_d), bf),
            vm((2 * n_routes, half_f), bf),
            vm((plane, nz, BLK, half_f), bf),
            vm((plane, nz, BLK, half_f), bf),
            vm((2, nz, plane, BLK, half_f), bf),
            vm((f_rows, nz * chunk), bf),
            vm((nz, 2, chunk, half_f), f32),
            vm((nz, chunk, half_f), f32),
            vm((nz, plane, BLK, half_f), bf),
            vm((nz, plane, BLK, half_f), bf),
            vm((nz, plane, BLK, half_f), bf),
            vm((2 * n_routes, half_f), f32),
            vm((2, n_routes, half_f), bf),
            dma((3,)), dma((3,)), dma((3,)),
            dma((2, steps, 2)), dma((2, steps, 2)), dma((2, steps, 2)), dma((2, steps, 2)),
            dma((nz,)), dma((nz,)), dma((nz,)),
            dma((1,)), dma((1,)), dma((1,)),
            dma((nz,)), dma((nz,)), dma((1,)),
            dma((nz,)), dma((nz,)),
            dma((nz,)), dma((nz,)),
            dma((nz,)), dma((nz,)), dma((nz,)),
            dma((nz,)), dma((nz,)), dma((1,)),
            dma((1,)), dma((1,)), dma((1,)), dma((1,)), dma((f // f_rows,)),
        ],
        compiler_params=pltpu.CompilerParams(
            collective_id=0, has_side_effects=True, vmem_limit_bytes=67043328
        ),
    )(og, hs, sid, weight)


def local(out_grad, hidden_act, gate_weight, routes, down_weight):
    groups = lax.axis_size("group")
    members = lax.axis_size("members")
    nz, ny = groups // NX, members // 2
    plane = NX * ny
    tok, d = out_grad.shape
    top, f = hidden_act.shape[1:]
    core = lax.rem(lax.axis_index("members"), 2)

    expert = routes.T.reshape(-1)
    earlier = jnp.arange(top * tok)[None, :] < jnp.arange(top * tok)[:, None]
    same = expert[None, :] == expert[:, None]
    rank = jnp.sum((same & earlier).astype(jnp.int32), axis=1)
    ex, ez, ey = expert // (nz * ny), (expert // ny) % nz, expert % ny
    slot = (ez * plane + ex * ny + ey) * BLK + core * PAD + rank
    sid = jnp.concatenate([slot.reshape(top, tok), jnp.full((top, tok), -1, jnp.int32)], axis=0)

    gate = gate_weight.astype(jnp.float32)
    hs = (gate[:, :, None] * hidden_act.astype(jnp.float32)).astype(jnp.bfloat16)
    hs = jnp.transpose(hs, (1, 0, 2)).reshape(top * tok, f)

    tiles = f // min(256, f // 2)
    weight = down_weight[0].reshape(tiles, f // tiles, d // 2)
    weight_grad, back = exchange(groups, members, out_grad, hs, sid, weight)
    weight_grad = weight_grad.reshape(1, f, d // 2)

    unscaled = jnp.transpose(back.reshape(2, top, tok, f // 2), (2, 1, 0, 3)).reshape(tok, top, f)
    wide = unscaled.astype(jnp.float32)
    hidden_grad = (gate[:, :, None] * wide).astype(jnp.bfloat16)
    gate_grad = jnp.sum(wide * hidden_act.astype(jnp.float32), axis=2)
    return weight_grad, hidden_grad, gate_grad


def solution(mesh):
    both = ("group", "members")
    return jax.shard_map(
        local,
        mesh=mesh,
        in_specs=(P(both, None), P(both, None, None), P(both, None), P(both, None), P(both, None, None)),
        out_specs=(P(both, None, None), P(both, None, None), P(both, None)),
        check_vma=False,
    )
```

```python
import functools

import jax
import jax.numpy as jnp
from jax import lax
from jax.experimental import pallas as pl
from jax.experimental.pallas import tpu as pltpu
from jax.sharding import PartitionSpec as P

MESH = pl.DeviceIdType.MESH
NX = 4
BLK = 16
CAP = 7
SPANS = ((0, 8), (8, 4), (12, 2))


class Place:
    def __init__(self, groups, members):
        self.nx = NX
        self.nz = groups // NX
        self.ny = members // 2
        self.plane = self.nx * self.ny
        g = lax.axis_index("group")
        m = lax.axis_index("members")
        self.x = g // self.nz
        self.z = lax.rem(g, self.nz)
        self.y = m // 2
        self.c = lax.rem(m, 2)
        self.a = self.x * self.ny + self.y

    def dev(self, x, z, y, c):
        return (x * self.nz + z, y * 2 + c)

    def sibling(self):
        return self.dev(self.x, self.z, self.y, 1 - self.c)

    def along_z(self, step):
        z = lax.rem(self.z + step + self.nz, self.nz)
        return z, self.dev(self.x, z, self.y, self.c)

    def in_plane(self, i):
        x = lax.rem(self.x + i // self.ny, self.nx)
        y = lax.rem(self.y + lax.rem(i, self.ny), self.ny)
        return x * self.ny + y, self.dev(x, self.z, y, self.c)

    def greet(self):
        barrier = pltpu.get_barrier_semaphore()
        pl.semaphore_signal(barrier, inc=1, device_id=self.sibling(), device_id_type=MESH)

        @pl.loop(1, self.nz)
        def _(j):
            pl.semaphore_signal(
                barrier, inc=1, device_id=self.along_z(j)[1], device_id_type=MESH
            )

        @pl.loop(1, self.plane)
        def _(i):
            pl.semaphore_signal(
                barrier, inc=1, device_id=self.in_plane(i)[1], device_id_type=MESH
            )

        pl.semaphore_wait(barrier, self.nz + self.plane - 1)


def remote(src, dst, ssem, rsem, device):
    return pltpu.make_async_remote_copy(
        src_ref=src, dst_ref=dst, send_sem=ssem, recv_sem=rsem, device_id=device, device_id_type=MESH
    )


def used(ref, span):
    at, n = SPANS[span]
    return ref.at[(slice(None),) * (len(ref.shape) - 2) + (slice(at, at + n),)]


def send_used(src, dst, ssem, rsem, device):
    for i in range(len(SPANS)):
        remote(used(src, i), used(dst, i), ssem.at[i], rsem.at[i], device).start()


def wait_used(blocks, sem):
    for i in range(len(SPANS)):
        pltpu.make_async_copy(used(blocks, i), used(blocks, i), sem.at[i]).wait()


def clear_rest(ref):
    rest = (slice(None),) * (len(ref.shape) - 2) + (slice(2 * CAP, BLK),)
    for i in range(ref.shape[0]):
        part = ref.at[i]
        part[rest[1:]] = jnp.zeros(part.shape[:-2] + (BLK - 2 * CAP, part.shape[-1]), ref.dtype)


def route_hits(ids, rows):
    parts = []
    for core in range(2):
        for k in range(ids.shape[1] // 2):
            hit = rows == ids[core, k : k + 1, :]
            parts.append(jnp.where(hit, 1.0, 0.0).astype(jnp.bfloat16))
    return jnp.concatenate(parts, axis=1)


def token_hits(ids, rows):
    parts = []
    for core in range(2):
        hit = rows == ids[core, 0:1, :]
        for k in range(1, ids.shape[1] // 2):
            hit = hit | (rows == ids[core, k : k + 1, :])
        parts.append(jnp.where(hit, 1.0, 0.0).astype(jnp.bfloat16))
    return jnp.concatenate(parts, axis=1)


def packed_slots(plane, shape, axis):
    i = lax.broadcasted_iota(jnp.int32, shape, axis)
    q = lax.shift_right_logical(i * 4682, 16)
    w = i - q * (2 * CAP)
    return q * BLK + w


def kernel(
    groups, members,
    og, hs, sid, w_in,
    wg, out,
    gat, ids, sb, rb, w, h0, hsend, hmid, hpk, hf, lt, part, got, ret, rmid, rpk, rr, acc, both,
    x_s, x_r, x_l, ag_s, ag_r, agm_s, agm_r,
    p_s, p_r, p_l, hp_s, hp_r, hp_l, hz_s, hz_r, hz_l, hx_s, hx_r,
    e_s, e_r, r_s, r_r, r_l, z_s, z_r, z_l, u_s, u_r, u_l, w_l, wg_l,
):
    me = Place(groups, members)
    nz, plane = me.nz, me.plane
    half_d = gat.shape[2]
    half_f = h0.shape[1]
    tok = og.shape[0]
    n_routes = hs.shape[0]
    z, c, a = me.z, me.c, me.a
    steps = nz // 2
    chunk = plane * BLK
    few = plane * 2 * CAP
    f32, bf = jnp.float32, jnp.bfloat16
    w_tiles, w_rows = w.shape[0], w.shape[1]

    me.greet()

    def cols(n, which):
        return pl.ds(pl.multiple_of(which * n, n), n)

    def block_of(o):
        down = lax.rem(o, 2) == 0
        step = lax.div(o + 1, 2)
        return lax.rem(jnp.where(down, z + step, z - step + nz), nz)

    own = [
        (og.at[:, cols(half_d, c)], gat.at[z, pl.ds(pl.multiple_of(c * tok, tok), tok)]),
        (sid, ids.at[z, c]),
        (hs.at[:, cols(half_f, c)], h0.at[pl.ds(pl.multiple_of(c * n_routes, n_routes), n_routes)]),
    ]
    away = [og.at[:, cols(half_d, 1 - c)], sid, hs.at[:, cols(half_f, 1 - c)]]
    give = [
        remote(src, dst, x_s.at[i], x_r.at[i], me.sibling())
        for i, (src, (_, dst)) in enumerate(zip(away, own))
    ]
    keep = [pltpu.make_async_copy(src, dst, x_l.at[i]) for i, (src, dst) in enumerate(own)]
    for op in give:
        op.start()
    for op in keep:
        op.start()
    for buf in (rb, hmid, rmid):
        clear_rest(buf)
    weights = pltpu.make_async_copy(w_in, w, w_l.at[0])
    weights.start()

    def ring(way, step, half):
        block = lax.rem(z - step + nz, nz) if way == 0 else lax.rem(z + step, nz)
        _, target = me.along_z(1 if way == 0 else -1)
        rows = gat.at[block, pl.ds(pl.multiple_of(half * tok, tok), tok)]
        table = ids.at[block, half]
        return (
            remote(rows, rows, ag_s.at[way, step, half], ag_r.at[way, step, half], target),
            remote(table, table, agm_s.at[way, step, half], agm_r.at[way, step, half], target),
        )

    def ring_start(way, step, half):
        for op in ring(way, step, half):
            op.start()

    def ring_arrive(way, step, half):
        for op in ring(way, step, half):
            op.wait_recv()

    keep[0].wait()
    keep[1].wait()
    ring_start(0, 0, c)
    ring_start(1, 0, c)
    give[0].wait_recv()
    give[1].wait_recv()
    ring_start(0, 0, 1 - c)
    ring_start(1, 0, 1 - c)

    def spread(block):
        rows = lax.broadcasted_iota(jnp.int32, (chunk, 1), 0) + z * chunk
        hits = token_hits(ids[block], rows)
        width = half_d // 7 if half_d % (7 * 128) == 0 else half_d
        for t in range(half_d // width):
            picked = jnp.dot(
                hits, gat[block, :, t * width : (t + 1) * width], preferred_element_type=f32
            )
            sb[block, :, :, t * width : (t + 1) * width] = picked.astype(bf).reshape(
                plane, BLK, width
            )

        @pl.loop(1, plane)
        def _(i):
            q, target = me.in_plane(i)
            send_used(sb.at[block, q], rb.at[block, a], p_s.at[block], p_r.at[block], target)

        pltpu.make_async_copy(sb.at[block, a], rb.at[block, a], p_l.at[block]).start()

    def spread_hidden():
        per_x = me.ny * nz * BLK

        @pl.loop(0, me.nx)
        def _(dx):
            row = lax.broadcasted_iota(jnp.int32, (per_x, 1), 0)
            xq = lax.rem(me.x + dx, me.nx)
            slot = lax.rem(row, BLK)
            zq = lax.rem(row // BLK, nz)
            yq = row // (BLK * nz)
            rows = zq * chunk + (xq * me.ny + yq) * BLK + slot
            hits = route_hits(ids[z], rows)
            picked = jnp.dot(hits, h0[...], preferred_element_type=f32)
            hsend[pl.ds(xq * me.ny, me.ny)] = picked.astype(bf).reshape(me.ny, nz, BLK, half_f)

        @pl.loop(1, plane)
        def _(i):
            q, target = me.in_plane(i)
            send_used(hsend.at[q], hmid.at[a], hp_s.at[0], hp_r.at[0], target)

        pltpu.make_async_copy(hsend.at[a], hmid.at[a], hp_l.at[0]).start()

    def hidden_arrive():
        wait_used(hmid.at[pl.ds(0, plane - 1)], hp_r.at[0])
        pltpu.make_async_copy(hsend.at[a], hmid.at[a], hp_l.at[0]).wait()

    def packing():
        slots = packed_slots(plane, (few, 1), 0)
        hit = slots == lax.broadcasted_iota(jnp.int32, (few, chunk), 1)
        return jnp.where(hit, 1.0, 0.0).astype(bf)

    def packed(rows):
        return jnp.dot(packing(), rows, preferred_element_type=f32).astype(bf)

    def hidden_hop(j):
        to, target = me.along_z(j)
        return remote(hpk.at[to], hf.at[c, z], hz_s.at[j], hz_r.at[j], target)

    def hidden_share(j):
        frm = lax.rem(z - j + nz, nz)
        return remote(hf.at[c, frm], hf.at[c, frm], hx_s.at[j], hx_r.at[j], me.sibling())

    def swap(b):
        return remote(
            part.at[b, 1 - c], got.at[b], e_s.at[b], e_r.at[b], me.sibling()
        )

    def multiply(o):
        b = block_of(o)
        wait_used(rb.at[b, pl.ds(0, plane - 1)], p_r.at[b])
        pltpu.make_async_copy(sb.at[b, a], rb.at[b, a], p_l.at[b]).wait()
        for t in range(w_tiles):
            at = t * w_rows
            part[b, at // half_f, :, at % half_f : at % half_f + w_rows] = lax.dot_general(
                rb[b].reshape(chunk, half_d),
                w[t],
                (((1,), (1,)), ((), ())),
                preferred_element_type=f32,
            )
        swap(b).start()

    def combine(o):
        b = block_of(o)
        swap(b).wait_recv()
        ret[b] = (part[b, c] + got[b]).astype(bf).reshape(plane, BLK, half_f)

        @pl.loop(1, plane)
        def _(i):
            q, target = me.in_plane(i)
            send_used(ret.at[b, q], rmid.at[b, a], r_s.at[b], r_r.at[b], target)

        pltpu.make_async_copy(ret.at[b, a], rmid.at[b, a], r_l.at[b]).start()

    def hop(b):
        return remote(rpk.at[b], rr.at[z], z_s.at[b], z_r.at[z], me.dev(me.x, b, me.y, c))

    def pass_on(o):
        b = block_of(o)
        wait_used(rmid.at[b, pl.ds(0, plane - 1)], r_r.at[b])
        pltpu.make_async_copy(ret.at[b, a], rmid.at[b, a], r_l.at[b]).wait()
        rpk[b] = packed(rmid[b].reshape(chunk, half_f))

        @pl.when(b != z)
        def _():
            hop(b).start()

        @pl.when(b == z)
        def _():
            pltpu.make_async_copy(rpk.at[b], rr.at[z], z_l.at[0]).start()

    spread(z)
    keep[2].wait()
    give[2].wait_recv()
    spread_hidden()
    weights.wait()

    @pl.loop(0, 2 * (steps - 1))
    def _(n):
        step = n // 2
        half = lax.rem(n, 2)
        lo = jnp.maximum(2 * step - 3, 0)
        hi = jnp.maximum(2 * step - 1, 0)
        ring_arrive(0, step, half)

        @pl.when(jnp.logical_or(step + 1 < steps - 1, half == 0))
        def _():
            ring_start(0, step + 1, half)

        ring_arrive(1, step, half)

        @pl.when(jnp.logical_or(step + 1 < steps - 1, half == 1))
        def _():
            ring_start(1, step + 1, half)

        @pl.when(half == 1)
        def _():
            @pl.loop(2 * step + 1, 2 * step + 3)
            def _(o):
                spread(block_of(o))

            @pl.loop(lo, hi)
            def _(o):
                combine(o)

        @pl.when(half == 0)
        def _():
            @pl.loop(lo, hi)
            def _(o):
                multiply(o)

    hidden_arrive()

    @pl.loop(1, nz)
    def _(j):
        to, _ = me.along_z(j)
        hpk[to] = packed(hmid[:, to].reshape(chunk, half_f))
        hidden_hop(j).start()

    hpk[z] = packed(hmid[:, z].reshape(chunk, half_f))
    pltpu.make_async_copy(hpk.at[z], hf.at[c, z], hz_l.at[0]).start()

    ring_arrive(0, steps - 1, 0)
    ring_arrive(1, steps - 1, 1)
    spread(block_of(nz - 1))
    first = max(2 * steps - 5, 0)

    @pl.loop(first, nz + 3)
    def _(i):
        @pl.when(i < nz)
        def _():
            multiply(i)

        @pl.when(jnp.logical_and(i > first, i < nz + 1))
        def _():
            combine(i - 1)

        @pl.when(i >= 3)
        def _():
            pass_on(i - 3)

    pltpu.make_async_copy(hpk.at[z], hf.at[c, z], hz_l.at[0]).wait()
    hidden_share(0).start()

    @pl.loop(1, nz)
    def _(j):
        hidden_hop(j).wait_recv()
        hidden_share(j).start()

    for step in range(steps):
        for way in range(2):
            for half in range(2):
                if step < steps - 1 or way == half:
                    for op in ring(way, step, half):
                        op.wait_send()

    @pl.loop(0, nz)
    def _(j):
        hidden_share(j).wait()

    f_rows = lt.shape[0]
    per_half = half_f // f_rows
    d_cols = 256

    @pl.loop(0, 2 * per_half)
    def _(i):
        h = i // per_half
        at = pl.multiple_of(lax.rem(i, per_half) * f_rows, f_rows)
        for b in range(nz):
            lt[:, b * chunk : (b + 1) * chunk] = lax.dot_general(
                hf[h, b, :, pl.ds(at, f_rows)],
                packing(),
                (((0,), (0,)), ((), ())),
                preferred_element_type=f32,
            ).astype(bf)

        @pl.loop(0, half_d // d_cols)
        def _(t):
            span = pl.ds(pl.multiple_of(t * d_cols, d_cols), d_cols)
            tile = jnp.dot(
                lt[...], rb[:, :, :, span].reshape(nz * chunk, d_cols), preferred_element_type=f32
            )
            gat[i, pl.ds(0, f_rows), span] = tile.astype(bf)

        pltpu.make_async_copy(
            gat.at[i, pl.ds(0, f_rows)], wg.at[pl.ds(i * f_rows, f_rows)], wg_l.at[i]
        ).start()

    acc[...] = jnp.zeros_like(acc)
    pltpu.make_async_copy(rpk.at[z], rr.at[z], z_l.at[0]).wait()

    @pl.loop(0, nz)
    def _(o):
        b = block_of(o)

        @pl.when(o > 0)
        def _():
            pltpu.make_async_copy(rr.at[b], rr.at[b], z_r.at[b]).wait()

        rows = packed_slots(plane, (few, 1), 0) + b * chunk
        hits = route_hits(ids[z], rows)
        acc[...] += lax.dot_general(
            hits,
            rr[b],
            (((0,), (0,)), ((), ())),
            preferred_element_type=f32,
        )

    both[...] = acc[...].astype(bf).reshape(both.shape)
    there = out.at[:, cols(half_f, c)]
    last = remote(both.at[1 - c], there, u_s.at[0], u_r.at[0], me.sibling())
    mine = pltpu.make_async_copy(both.at[c], there, u_l.at[0])
    last.start()
    mine.start()

    @pl.loop(0, nz)
    def _(b):
        for buf, sem in ((sb, p_s), (ret, r_s)):
            wait_used(buf.at[b, pl.ds(0, plane - 1)], sem.at[b])
        swap(b).wait_send()

        @pl.when(b != z)
        def _():
            hop(b).wait_send()

    @pl.loop(1, nz)
    def _(j):
        hidden_hop(j).wait_send()

    wait_used(hsend.at[pl.ds(0, plane - 1)], hp_s.at[0])
    for op in give:
        op.wait_send()

    @pl.loop(0, 2 * per_half)
    def _(i):
        pltpu.make_async_copy(
            gat.at[i, pl.ds(0, f_rows)], wg.at[pl.ds(i * f_rows, f_rows)], wg_l.at[i]
        ).wait()

    mine.wait()
    last.wait()


def exchange(groups, members, og, hs, sid, weight):
    nz, ny = groups // NX, members // 2
    plane = NX * ny
    tok, d = og.shape
    n_routes, f = hs.shape
    half_d, half_f = d // 2, f // 2
    chunk = plane * BLK
    few = plane * 2 * CAP
    dma = pltpu.SemaphoreType.DMA
    any_ = pl.BlockSpec(memory_space=pl.ANY)
    bf, f32 = jnp.bfloat16, jnp.float32
    steps = nz // 2
    w_rows = min(256, half_f)
    f_rows = min(256, half_f)
    vm = pltpu.VMEM
    spans = len(SPANS)
    return pl.pallas_call(
        functools.partial(kernel, groups, members),
        name="exchange",
        out_shape=(
            jax.ShapeDtypeStruct((f, half_d), bf),
            jax.ShapeDtypeStruct((n_routes, f), bf),
        ),
        in_specs=[any_] * 4,
        out_specs=(any_,) * 2,
        scratch_shapes=[
            vm((nz, 2 * tok, half_d), bf),
            vm((nz, 2) + sid.shape, jnp.int32),
            vm((nz, plane, BLK, half_d), bf),
            vm((nz, plane, BLK, half_d), bf),
            vm((f // w_rows, w_rows, half_d), bf),
            vm((2 * n_routes, half_f), bf),
            vm((plane, nz, BLK, half_f), bf),
            vm((plane, nz, BLK, half_f), bf),
            vm((nz, few, half_f), bf),
            vm((2, nz, few, half_f), bf),
            vm((f_rows, nz * chunk), bf),
            vm((nz, 2, chunk, half_f), f32),
            vm((nz, chunk, half_f), f32),
            vm((nz, plane, BLK, half_f), bf),
            vm((nz, plane, BLK, half_f), bf),
            vm((nz, few, half_f), bf),
            vm((nz, few, half_f), bf),
            vm((2 * n_routes, half_f), f32),
            vm((2, n_routes, half_f), bf),
            dma((3,)), dma((3,)), dma((3,)),
            dma((2, steps, 2)), dma((2, steps, 2)), dma((2, steps, 2)), dma((2, steps, 2)),
            dma((nz, spans)), dma((nz, spans)), dma((nz,)),
            dma((1, spans)), dma((1, spans)), dma((1,)),
            dma((nz,)), dma((nz,)), dma((1,)),
            dma((nz,)), dma((nz,)),
            dma((nz,)), dma((nz,)),
            dma((nz, spans)), dma((nz, spans)), dma((nz,)),
            dma((nz,)), dma((nz,)), dma((1,)),
            dma((1,)), dma((1,)), dma((1,)), dma((1,)), dma((f // f_rows,)),
        ],
        compiler_params=pltpu.CompilerParams(
            collective_id=0, has_side_effects=True, vmem_limit_bytes=67043328
        ),
    )(og, hs, sid, weight)


def local(out_grad, hidden_act, gate_weight, routes, down_weight):
    groups = lax.axis_size("group")
    members = lax.axis_size("members")
    nz, ny = groups // NX, members // 2
    plane = NX * ny
    tok, d = out_grad.shape
    top, f = hidden_act.shape[1:]
    core = lax.rem(lax.axis_index("members"), 2)

    expert = routes.T.reshape(-1)
    earlier = jnp.arange(top * tok)[None, :] < jnp.arange(top * tok)[:, None]
    same = expert[None, :] == expert[:, None]
    rank = jnp.sum((same & earlier).astype(jnp.int32), axis=1)
    ex, ez, ey = expert // (nz * ny), (expert // ny) % nz, expert % ny
    slot = (ez * plane + ex * ny + ey) * BLK + core * CAP + rank
    sid = jnp.concatenate([slot.reshape(top, tok), jnp.full((top, tok), -1, jnp.int32)], axis=0)

    gate = gate_weight.astype(jnp.float32)
    hs = (gate[:, :, None] * hidden_act.astype(jnp.float32)).astype(jnp.bfloat16)
    hs = jnp.transpose(hs, (1, 0, 2)).reshape(top * tok, f)

    tiles = f // min(256, f // 2)
    weight = down_weight[0].reshape(tiles, f // tiles, d // 2)
    weight_grad, back = exchange(groups, members, out_grad, hs, sid, weight)
    weight_grad = weight_grad.reshape(1, f, d // 2)

    unscaled = jnp.transpose(back.reshape(top, tok, f), (1, 0, 2))
    wide = unscaled.astype(jnp.float32)
    hidden_grad = (gate[:, :, None] * wide).astype(jnp.bfloat16)
    gate_grad = jnp.sum(wide * hidden_act.astype(jnp.float32), axis=2)
    return weight_grad, hidden_grad, gate_grad


def solution(mesh):
    both = ("group", "members")
    return jax.shard_map(
        local,
        mesh=mesh,
        in_specs=(P(both, None), P(both, None, None), P(both, None), P(both, None), P(both, None, None)),
        out_specs=(P(both, None, None), P(both, None, None), P(both, None)),
        check_vma=False,
    )
```
